32 devices in a mesh: row: 8 (over z, y), col: 4 (over x, core).
Axes of the slice: x: 2, y: 2, z: 4, core: 2. Of those that a mesh axis runs over, the one named last changes fastest.
Arguments:
- candidates: float32 [512, 32768], P('col', 'row'), may hold values from -64 to 64
- trailing: float32 [512, 32768], P('col', 'row'), may hold values from -64 to 64
- pivots: int32 [64], replicated, may hold values from 0 to 511, as said below
Outputs:
- r_panel: float32 [64, 64], replicated
- r_trail: float32 [64, 512], P(None, 'col')
- basis: float32 [64, 32768], P(None, 'row')
- trailing_next: float32 [512, 32768], P('col', 'row')
The draws below stay inside these ranges and needn't reach their ends.
Inputs may be any that keep to these rules, and one draw needn't show every extreme that they name: `pivots`: 64 distinct column numbers; one block of 128 consecutive columns (those of one index of col) holds exactly 32 of them and no block holds more.
All inputs are finite; a program needn't handle non-finite values.
Results may differ from the reference program's by a relative error of at most 0.0003.
Values sent between devices are 32-bit elements; how exact they have to be, the bound alone decides.
A program may use at most 64 MiB of HBM per device.

```python
import jax
import jax.numpy as jnp
from jax import lax

ROWS_DEV = 4096
CAND_DEV = 128
K = 64
TRAIL = 512
ROWS = 32768
N_ROW = 8
N_COL = 4


def drawn_all(key):
    rows_all = ROWS_DEV * N_ROW
    cand_all = CAND_DEV * N_COL
    keys = [jax.random.fold_in(key, 7100 + i) for i in range(12)]
    heavy = jax.random.randint(keys[0], (), 0, N_COL)
    own_cols = jax.random.permutation(keys[1], CAND_DEV)[:K // 2] + heavy * CAND_DEV
    spread = jax.random.permutation(keys[2], (N_COL - 1) * CAND_DEV)[:K - K // 2]
    spread_dev = spread // CAND_DEV
    spread_dev = spread_dev + (spread_dev >= heavy).astype(jnp.int32)
    other_cols = spread_dev * CAND_DEV + spread % CAND_DEV
    chosen = jnp.concatenate([own_cols.astype(jnp.int32), other_cols.astype(jnp.int32)])
    chosen = chosen[jax.random.permutation(keys[3], K)].astype(jnp.int32)
    noise = jax.random.truncated_normal(keys[4], -6.0, 6.0, (cand_all, rows_all), jnp.float32)
    ramp = jnp.arange(rows_all, dtype=jnp.float32) / jnp.float32(rows_all - 1)
    rise = jnp.exp(jnp.log(3.0) * ramp)
    row_scale = jnp.exp(jax.random.uniform(keys[5], (rows_all,), jnp.float32, jnp.log(0.3), jnp.log(3.0)))
    col_scale = jnp.exp(jax.random.uniform(keys[6], (cand_all,), jnp.float32, jnp.log(0.3), jnp.log(3.0)))
    base = noise
    cands = jnp.clip(base * (row_scale * rise)[None, :] * col_scale[:, None], -64.0, 64.0)
    panel = jnp.take(cands, chosen, axis=0)
    mixing = jax.random.truncated_normal(keys[9], -3.0, 3.0, (TRAIL, K), jnp.float32)
    extra = jax.random.truncated_normal(keys[10], -6.0, 6.0, (TRAIL, rows_all), jnp.float32)
    mixed = jnp.dot(mixing, panel, preferred_element_type=jnp.float32, precision=lax.Precision.HIGHEST)
    trail = jnp.clip(extra + mixed / jnp.sqrt(jnp.float32(K)), -64.0, 64.0)
    return (cands, trail, chosen)


def draw_candidates(key, part):
    return drawn_all(key)[0]


def draw_trailing(key, part):
    return drawn_all(key)[1]


def draw_pivots(key, part):
    return drawn_all(key)[2]


def setup_inputs(seed: int = 0) -> dict:
    splits = jax.random.split(jax.random.key(seed), 4)
    candidates = draw_candidates(jax.random.fold_in(splits[3], 71), 0)
    trailing = draw_trailing(jax.random.fold_in(splits[3], 71), 0)
    pivots = draw_pivots(jax.random.fold_in(splits[3], 71), 0)
    return dict(candidates=candidates, trailing=trailing, pivots=pivots)


def reference(candidates, trailing, pivots):
    panel = jnp.take(candidates, pivots, axis=0)
    gram = jnp.dot(panel.astype(jnp.float32), panel.T.astype(jnp.float32), preferred_element_type=jnp.float32, precision=lax.Precision.HIGHEST)
    upper = jnp.linalg.cholesky(gram).T
    ortho = jax.scipy.linalg.solve_triangular(upper, panel, trans=1, lower=False)
    projected = jnp.dot(ortho.astype(jnp.float32), trailing.T.astype(jnp.float32), preferred_element_type=jnp.float32, precision=lax.Precision.HIGHEST)
    trailing_next = trailing - jnp.dot(projected.T.astype(jnp.float32), ortho.astype(jnp.float32), preferred_element_type=jnp.float32, precision=lax.Precision.HIGHEST)
    root_rows = jnp.sqrt(jnp.float32(ROWS))
    return (upper / root_rows, projected / root_rows, ortho * root_rows, trailing_next)
```

```python
import functools

import jax
import jax.numpy as jnp
from jax import lax
from jax.experimental import pallas as pl
from jax.experimental.pallas import tpu as pltpu
from jax.sharding import PartitionSpec as P

MESH = pl.DeviceIdType.MESH
CORES = 2
F32 = jnp.float32
BF16 = jnp.bfloat16
BLOCK = 16
PIECES = (1, 4, 3)
UPDATE_CHUNKS = 4
GRANT = 24 * 2**20


def split(x):
    high = x.astype(BF16)
    return high, (x - high.astype(F32)).astype(BF16)


def dot(a, b):
    return jnp.dot(a, b, preferred_element_type=F32)


def exact(a, b):
    return jnp.dot(a, b, preferred_element_type=F32, precision=lax.Precision.HIGHEST)


def dot_t(a, b):
    return lax.dot_general(a, b, (((1,), (1,)), ((), ())), preferred_element_type=F32)


def iota(shape, dim):
    return lax.broadcasted_iota(jnp.int32, shape, dim)


def eliminate(state, start):
    rest = state
    tile = iota((BLOCK, state.shape[1]), 0)
    columns = [jnp.broadcast_to(rest[:, start + c:start + c + 1], rest.shape) for c in range(BLOCK)]
    for c in range(BLOCK):
        inverse = 1.0 / columns[c][c:c + 1]
        below = jnp.where(tile > c, columns[c][:BLOCK], 0.0)
        if rest.shape[0] > BLOCK:
            below = jnp.concatenate([below, columns[c][BLOCK:]], axis=0)
        for e in range(c + 1, BLOCK):
            columns[e] = columns[e] - below * (columns[e][c:c + 1] * inverse)
        rest = rest - below * (rest[c:c + 1] * inverse)
    return rest[:BLOCK], rest[BLOCK:]


def gather_kernel(
    n_row, n_col, windows, root_rows,
    piv_hbm, cand_hbm, trail_hbm,
    rp_ref, rt_ref, left_ref, high_ref, low_ref, trail,
    piv_ref, cand, bufs, grams, csend, crecv, cfull,
    piv_sem, cand_sem, trail_sem,
    xs, xr, ss, sr, fs, fr, gs, gr, cs, cr, as_, ar,
    up_sem, down_sem, mate_sem,
):
    row = lax.axis_index("row")
    col = lax.axis_index("col")
    n_x = n_col // CORES
    x = col // CORES
    core = lax.rem(col, CORES)
    sibling = x * CORES + (1 - core)
    count = piv_ref.shape[1]
    cap = count // 2
    cand_count = cand.shape[0]

    def x_peer(d):
        return lax.rem(x + d, n_x) * CORES + core

    def x_source(d):
        return lax.rem(x + n_x - d, n_x) * CORES + core

    def row_peer(d):
        return lax.rem(row + d, n_row)

    piv_copy = pltpu.make_async_copy(piv_hbm, piv_ref, piv_sem)
    piv_copy.start()
    cand_copies = []
    for k, (first, width) in enumerate(windows):
        window = pl.ds(first, width)
        copy = pltpu.make_async_copy(cand_hbm.at[:, window], cand.at[:, window], cand_sem.at[k])
        copy.start()
        cand_copies.append(copy)
    trail_copy = pltpu.make_async_copy(trail_hbm, trail, trail_sem)

    barrier = pltpu.get_barrier_semaphore()
    pl.semaphore_signal(barrier, inc=1, device_id=(row, sibling), device_id_type=MESH)
    for d in range(1, n_x):
        pl.semaphore_signal(barrier, inc=1, device_id=(row, x_peer(d)), device_id_type=MESH)
    mate = row + 1 - 2 * lax.rem(row, 2)
    has_below, has_above = row >= 2, row < n_row - 2

    def signal(semaphore, to):
        pl.semaphore_signal(semaphore, inc=1, device_id=(to, col), device_id_type=MESH)

    signal(barrier, mate)
    pl.when(has_below)(lambda: signal(barrier, row - 2))
    pl.when(has_above)(lambda: signal(barrier, row + 2))

    piv_copy.wait()
    piv_lane = jnp.broadcast_to(piv_ref[...].astype(F32), (count, count))
    rows_i, lanes_i = iota((count, count), 0), iota((count, count), 1)
    piv_sub = jnp.sum(jnp.where(rows_i == lanes_i, piv_lane, 0.0), axis=1, keepdims=True)
    owner_lane = jnp.zeros((count, count), F32)
    owner_sub = jnp.zeros((count, 1), F32)
    for s in range(1, n_col):
        owner_lane += (piv_lane >= s * cand_count).astype(F32)
        owner_sub += (piv_sub >= s * cand_count).astype(F32)
    same = jnp.broadcast_to(owner_sub, (count, count)) == owner_lane
    rank_sub = jnp.sum(jnp.where(same & (lanes_i < rows_i), 1.0, 0.0), axis=1, keepdims=True)
    rank_lane = jnp.sum(jnp.where(same & (rows_i < lanes_i), 1.0, 0.0), axis=0, keepdims=True)
    slot_sub = (owner_sub * cap + rank_sub).astype(jnp.int32)
    slot_lane = (owner_lane[:1] * cap + rank_lane).astype(jnp.int32)
    expand = (slot_sub == iota((count, n_col * cap), 1)).astype(F32).astype(BF16)
    to_slot = (slot_lane == col * cap + iota((cap, count), 0)).astype(F32).astype(BF16)
    to_cand = (piv_sub.astype(jnp.int32) == col * cand_count + iota((count, cand_count), 1))
    pick = dot(to_slot, to_cand.astype(F32).astype(BF16)).astype(BF16)

    def remote(src, dst, send, recv, device):
        return pltpu.make_async_remote_copy(
            src_ref=src, dst_ref=dst, send_sem=send, recv_sem=recv,
            device_id=device, device_id_type=MESH,
        )

    sends = []
    for k, (first, width) in enumerate(windows):
        window = pl.ds(first, width)
        cand_copies[k].wait()
        high, low = split(cand[:, window])
        bufs[col, :, window] = dot(pick, high) + dot(pick, low)
        if k == 0:
            pl.semaphore_wait(barrier, n_x + 1 + has_below.astype(jnp.int32) + has_above.astype(jnp.int32))
        mine = bufs.at[col, :, window]
        for d in range(1, n_x):
            copy = remote(mine, mine, xs.at[k, d - 1], xr.at[k, d - 1], (row, x_peer(d)))
            copy.start()
            sends.append(copy)
        copy = remote(mine, mine, ss.at[k], sr.at[k], (row, sibling))
        copy.start()
        sends.append(copy)

    trail_copy.start()
    @pl.when(jnp.logical_not(has_below))
    def _():
        signal(up_sem, row + 2)

    @pl.when(jnp.logical_not(has_above))
    def _():
        signal(down_sem, row - 2)

    @pl.when(has_below)
    def _():
        pl.semaphore_wait(up_sem, 1)
        pl.when(has_above)(lambda: signal(up_sem, row + 2))

    @pl.when(has_above)
    def _():
        pl.semaphore_wait(down_sem, 1)
        pl.when(has_below)(lambda: signal(down_sem, row - 2))

    signal(mate_sem, mate)
    tc = trail.shape[0]
    acc = jnp.zeros((count, count + tc), F32)
    trail_copy.wait()
    for k, (first, width) in enumerate(windows):
        window = pl.ds(first, width)
        for d in range(1, n_x):
            theirs = bufs.at[x_source(d), :, window]
            remote(theirs, theirs, xs.at[k, d - 1], xr.at[k, d - 1], (row, x_peer(d))).wait_recv()
            copy = remote(theirs, theirs, fs.at[k, d - 1], fr.at[k, d - 1], (row, sibling))
            copy.start()
            sends.append(copy)
        t_high, t_low = split(trail[:, window])
        arrived = bufs.at[sibling, :, window]
        remote(arrived, arrived, ss.at[k], sr.at[k], (row, sibling)).wait_recv()
        for d in range(1, n_x):
            arrived = bufs.at[lax.rem(x + n_x - d, n_x) * CORES + (1 - core), :, window]
            remote(arrived, arrived, fs.at[k, d - 1], fr.at[k, d - 1], (row, sibling)).wait_recv()
        high, low = split(bufs[:, :, window].reshape(n_col * cap, width))
        p_high = dot(expand, high).astype(BF16)
        p_low = dot(expand, low).astype(BF16)
        high_ref[:, window] = p_high
        low_ref[:, window] = p_low
        both = dot_t(jnp.concatenate([p_high, p_low], axis=0), jnp.concatenate([p_high, t_high], axis=0))
        acc += both[:count] + both[count:] + dot_t(p_high, jnp.concatenate([p_low, t_low], axis=0))

    pl.semaphore_wait(mate_sem, 1)
    part = count // n_row
    half = count // 2
    for r in range(n_row):
        csend[r] = acc[r * part:(r + 1) * part, count:]
    crecv[row] = csend[row]
    for d in range(1, n_row):
        copy = remote(csend.at[row_peer(d)], crecv.at[row], cs.at[d - 1], cr.at[d - 1], (row_peer(d), col))
        copy.start()
        sends.append(copy)

    grams[row] = jnp.concatenate([acc[:half, :count], acc[half:, :count]], axis=1)
    for d in range(1, n_row):
        mine = grams.at[row]
        copy = remote(mine, mine, gs.at[d - 1], gr.at[d - 1], (row_peer(d), col))
        copy.start()
        sends.append(copy)
    def source(d):
        return lax.rem(row + n_row - d, n_row)

    for d in range(1, n_row):
        arrived = crecv.at[source(d)]
        remote(arrived, arrived, cs.at[d - 1], cr.at[d - 1], (row_peer(d), col)).wait_recv()
    cfull[row] = jnp.sum(crecv[...], axis=0)
    for d in range(1, n_row):
        mine = cfull.at[row]
        copy = remote(mine, mine, as_.at[d - 1], ar.at[d - 1], (row_peer(d), col))
        copy.start()
        sends.append(copy)
    for d in range(1, n_row):
        arrived = grams.at[source(d)]
        remote(arrived, arrived, gs.at[d - 1], gr.at[d - 1], (row_peer(d), col)).wait_recv()
    packed = jnp.sum(grams[...], axis=0)
    gram = jnp.concatenate([packed[:, :count], packed[:, count:]], axis=0)
    unit = jnp.where(rows_i == lanes_i, 1.0, 0.0)
    state = jnp.concatenate([gram, unit], axis=1)
    done = []
    for start in range(0, count, BLOCK):
        block, state = eliminate(state, start)
        done.append(block)
    state = jnp.concatenate(done, axis=0)
    wide = (count, 2 * count)
    diagonal = jnp.sum(jnp.where(iota(wide, 0) == iota(wide, 1), state, 0.0), axis=1, keepdims=True)
    scaled = state / jnp.sqrt(diagonal)
    factor = jnp.where(iota(wide, 0) <= iota(wide, 1), scaled, 0.0)[:, :count]
    inverse = scaled[:, count:]
    rp_ref[...] = factor * (1.0 / root_rows)
    for d in range(1, n_row):
        arrived = cfull.at[source(d)]
        remote(arrived, arrived, as_.at[d - 1], ar.at[d - 1], (row_peer(d), col)).wait_recv()
    projected = exact(inverse, cfull[...].reshape(count, tc))
    weights = exact(inverse.T, projected).T
    rt_ref[...] = projected * (1.0 / root_rows)
    left_high, left_low = split(jnp.concatenate([inverse * root_rows, weights], axis=0))
    left_ref[...] = jnp.concatenate([left_high, left_low, left_high], axis=1)
    for copy in sends:
        copy.wait_send()


def update_kernel(
    chunks,
    rp_ref, rt_ref, left_ref, high, low, trail,
    rp_hbm, rt_hbm, basis_hbm, next_hbm,
    basis, after,
    small_sem, out_sem,
):
    stores = []
    for i, (src, dst) in enumerate(((rp_ref, rp_hbm), (rt_ref, rt_hbm))):
        copy = pltpu.make_async_copy(src, dst, small_sem.at[i])
        copy.start()
        stores.append(copy)
    count = high.shape[0]
    width = trail.shape[1] // chunks
    left = left_ref[...]
    for k in range(chunks):
        window = pl.ds(k * width, width)
        p_high = high[:, window]
        result = dot(left, jnp.concatenate([p_high, p_high, low[:, window]], axis=0))
        basis[:, window] = result[:count]
        after[:, window] = trail[:, window] - result[count:]
        for i, (src, dst) in enumerate(((basis, basis_hbm), (after, next_hbm))):
            copy = pltpu.make_async_copy(src.at[:, window], dst.at[:, window], out_sem.at[k, i])
            copy.start()
            stores.append(copy)
    for copy in stores:
        copy.wait()


def solution(mesh):
    n_row, n_col = mesh.shape["row"], mesh.shape["col"]
    n_x = n_col // CORES
    chunks = len(PIECES)
    update_chunks = UPDATE_CHUNKS

    def on_device(candidates, trailing, pivots):
        cand_count, rows = candidates.shape
        tc = trailing.shape[0]
        count = pivots.shape[0]
        cap = count // 2
        eighth = rows // 8
        windows = tuple((sum(PIECES[:k]) * eighth, PIECES[k] * eighth) for k in range(chunks))
        part = count // n_row
        vmem = pl.BlockSpec(memory_space=pltpu.VMEM)
        hbm = pl.BlockSpec(memory_space=pltpu.HBM)
        dma = pltpu.SemaphoreType.DMA
        root_rows = float(rows * n_row) ** 0.5
        handed = pl.pallas_call(
            functools.partial(gather_kernel, n_row, n_col, windows, root_rows),
            name="gather",
            out_shape=(
                jax.ShapeDtypeStruct((count, count), F32),
                jax.ShapeDtypeStruct((count, tc), F32),
                jax.ShapeDtypeStruct((count + tc, 3 * count), BF16),
                jax.ShapeDtypeStruct((count, rows), BF16),
                jax.ShapeDtypeStruct((count, rows), BF16),
                jax.ShapeDtypeStruct((tc, rows), F32),
            ),
            in_specs=[hbm, hbm, hbm],
            out_specs=(vmem,) * 6,
            scratch_shapes=[
                pltpu.VMEM((1, count), jnp.int32),
                pltpu.VMEM((cand_count, rows), F32),
                pltpu.VMEM((n_col, cap, rows), F32),
                pltpu.VMEM((n_row, count // 2, 2 * count), F32),
                pltpu.VMEM((n_row, part, tc), F32),
                pltpu.VMEM((n_row, part, tc), F32),
                pltpu.VMEM((n_row, part, tc), F32),
                dma, dma((chunks,)), dma,
                dma((chunks, n_x - 1)), dma((chunks, n_x - 1)),
                dma((chunks,)), dma((chunks,)),
                dma((chunks, n_x - 1)), dma((chunks, n_x - 1)),
                dma((n_row - 1,)), dma((n_row - 1,)),
                dma((n_row - 1,)), dma((n_row - 1,)),
                dma((n_row - 1,)), dma((n_row - 1,)),
            ] + [pltpu.SemaphoreType.REGULAR] * 3,
            compiler_params=pltpu.CompilerParams(
                collective_id=0, has_side_effects=True, vmem_limit_bytes=GRANT,
            ),
        )(*[pltpu.with_memory_space_constraint(a, pltpu.HBM) for a in (pivots.reshape(1, count), candidates, trailing)])
        return pl.pallas_call(
            functools.partial(update_kernel, update_chunks),
            name="update",
            out_shape=(
                jax.ShapeDtypeStruct((count, count), F32),
                jax.ShapeDtypeStruct((count, tc), F32),
                jax.ShapeDtypeStruct((count, rows), F32),
                jax.ShapeDtypeStruct((tc, rows), F32),
            ),
            in_specs=[vmem] * 6,
            out_specs=(hbm,) * 4,
            scratch_shapes=[
                pltpu.VMEM((count, rows), F32),
                pltpu.VMEM((tc, rows), F32),
                dma((2,)), dma((update_chunks, 2)),
            ],
            compiler_params=pltpu.CompilerParams(vmem_limit_bytes=GRANT),
        )(*handed)

    placed = (P("col", "row"), P("col", "row"), P())
    return jax.shard_map(
        on_device,
        mesh=mesh,
        in_specs=placed,
        out_specs=(P(), P(None, "col"), P(None, "row"), P("col", "row")),
        check_vma=False,
    )
```

```python
import functools

import jax
import jax.numpy as jnp
from jax import lax
from jax.experimental import pallas as pl
from jax.experimental.pallas import tpu as pltpu
from jax.sharding import PartitionSpec as P

MESH = pl.DeviceIdType.MESH
CORES = 2
F32 = jnp.float32
BF16 = jnp.bfloat16
BLOCK = 16
PIECES = (1, 4, 3)
UPDATE_CHUNKS = 4
GRANT = 24 * 2**20


def split(x):
    high = x.astype(BF16)
    return high, (x - high.astype(F32)).astype(BF16)


def dot(a, b):
    return jnp.dot(a, b, preferred_element_type=F32)


def exact(a, b):
    return jnp.dot(a, b, preferred_element_type=F32, precision=lax.Precision.HIGHEST)


def dot_t(a, b):
    return lax.dot_general(a, b, (((1,), (1,)), ((), ())), preferred_element_type=F32)


def iota(shape, dim):
    return lax.broadcasted_iota(jnp.int32, shape, dim)


def eliminate(state, start):
    rest = state
    tile = iota((BLOCK, state.shape[1]), 0)
    columns = [jnp.broadcast_to(rest[:, start + c:start + c + 1], rest.shape) for c in range(BLOCK)]
    for c in range(BLOCK):
        inverse = 1.0 / columns[c][c:c + 1]
        below = jnp.where(tile > c, columns[c][:BLOCK], 0.0)
        if rest.shape[0] > BLOCK:
            below = jnp.concatenate([below, columns[c][BLOCK:]], axis=0)
        for e in range(c + 1, BLOCK):
            columns[e] = columns[e] - below * (columns[e][c:c + 1] * inverse)
        rest = rest - below * (rest[c:c + 1] * inverse)
    return rest[:BLOCK], rest[BLOCK:]


def gather_kernel(
    n_row, n_col, windows, root_rows, low, heavy,
    piv_hbm, cand_hbm, trail_hbm,
    rp_ref, rt_ref, left_ref, high_ref, low_ref, trail,
    piv_ref, cand, bufs, grams, csend, crecv, cfull,
    piv_sem, cand_sem, trail_sem,
    xs, xr, ss, sr, fs, fr, exs, exr, ess, esr, gs, gr, cs, cr, as_, ar,
    up_sem, down_sem, mate_sem,
):
    row = lax.axis_index("row")
    col = lax.axis_index("col")
    n_x = n_col // CORES
    x = col // CORES
    core = lax.rem(col, CORES)
    sibling = x * CORES + (1 - core)
    count = piv_ref.shape[1]
    cand_count = cand.shape[0]
    slots = bufs.shape[0]
    extra = pl.ds(n_col * low, slots - n_col * low)

    def x_peer(d):
        return lax.rem(x + d, n_x) * CORES + core

    def x_source(d):
        return lax.rem(x + n_x - d, n_x) * CORES + core

    def row_peer(d):
        return lax.rem(row + d, n_row)

    barrier = pltpu.get_barrier_semaphore()
    pl.semaphore_signal(barrier, inc=1, device_id=(row, sibling), device_id_type=MESH)
    for d in range(1, n_x):
        pl.semaphore_signal(barrier, inc=1, device_id=(row, x_peer(d)), device_id_type=MESH)
    mate = row + 1 - 2 * lax.rem(row, 2)
    has_below, has_above = row >= 2, row < n_row - 2

    def signal(semaphore, to):
        pl.semaphore_signal(semaphore, inc=1, device_id=(to, col), device_id_type=MESH)

    signal(barrier, mate)
    pl.when(has_below)(lambda: signal(barrier, row - 2))
    pl.when(has_above)(lambda: signal(barrier, row + 2))

    piv_copy = pltpu.make_async_copy(piv_hbm, piv_ref, piv_sem)
    piv_copy.start()
    cand_copies = []
    for k, (first, width) in enumerate(windows):
        window = pl.ds(first, width)
        copy = pltpu.make_async_copy(cand_hbm.at[:, window], cand.at[:, window], cand_sem.at[k])
        copy.start()
        cand_copies.append(copy)
    trail_copy = pltpu.make_async_copy(trail_hbm, trail, trail_sem)

    piv_copy.wait()
    piv_lane = jnp.broadcast_to(piv_ref[...].astype(F32), (count, count))
    rows_i, lanes_i = iota((count, count), 0), iota((count, count), 1)
    piv_sub = jnp.sum(jnp.where(rows_i == lanes_i, piv_lane, 0.0), axis=1, keepdims=True)
    owner_lane = jnp.zeros((count, count), F32)
    owner_sub = jnp.zeros((count, 1), F32)
    for s in range(1, n_col):
        owner_lane += (piv_lane >= s * cand_count).astype(F32)
        owner_sub += (piv_sub >= s * cand_count).astype(F32)
    same = jnp.broadcast_to(owner_sub, (count, count)) == owner_lane
    rank_sub = jnp.sum(jnp.where(same & (lanes_i < rows_i), 1.0, 0.0), axis=1, keepdims=True)
    rank_lane = jnp.sum(jnp.where(same & (rows_i < lanes_i), 1.0, 0.0), axis=0, keepdims=True)
    def slot_of(owner, rank):
        return jnp.where(rank < low, owner * low + rank, rank + (n_col - 1) * low).astype(jnp.int32)

    expand = (slot_of(owner_sub, rank_sub) == iota((count, slots), 1)).astype(F32).astype(BF16)
    own = iota((slots - (n_col - 1) * low, count), 0)
    own = jnp.where(own < low, own + col * low, own + (n_col - 1) * low)
    to_slot = (slot_of(owner_lane[:1], rank_lane) == own).astype(F32).astype(BF16)
    to_cand = (piv_sub.astype(jnp.int32) == col * cand_count + iota((count, cand_count), 1))
    pick = dot(to_slot, to_cand.astype(F32).astype(BF16)).astype(BF16)

    def remote(src, dst, send, recv, device):
        return pltpu.make_async_remote_copy(
            src_ref=src, dst_ref=dst, send_sem=send, recv_sem=recv,
            device_id=device, device_id_type=MESH,
        )

    def mains(owner, window):
        return bufs.at[pl.ds(pl.multiple_of(owner * low, low), low), window]

    sends = []
    if heavy is not None:
        heavy_x, heavy_core = heavy // CORES, heavy % CORES
        is_heavy = col == heavy
        is_relay = (core == heavy_core) & (x != heavy_x)
        is_told = core == heavy_core

    for k, (first, width) in enumerate(windows):
        window = pl.ds(first, width)
        cand_copies[k].wait()
        high, low_part = split(cand[:, window])
        picked = dot(pick, high) + dot(pick, low_part)
        bufs[pl.ds(pl.multiple_of(col * low, low), low), window] = picked[:low]
        if k == 0:
            pl.semaphore_wait(barrier, n_x + 1 + has_below.astype(jnp.int32) + has_above.astype(jnp.int32))
        mine = mains(col, window)
        for d in range(1, n_x):
            copy = remote(mine, mine, xs.at[k, d - 1], xr.at[k, d - 1], (row, x_peer(d)))
            copy.start()
            sends.append(copy)
        if heavy is not None:
            @pl.when(is_heavy)
            def _():
                bufs[extra, window] = picked[low:]
                more = bufs.at[extra, window]
                for d in range(1, n_x):
                    remote(more, more, exs.at[k, d - 1], exr.at[k], (row, x_peer(d))).start()
                remote(more, more, ess.at[k], esr.at[k], (row, sibling)).start()
        copy = remote(mine, mine, ss.at[k], sr.at[k], (row, sibling))
        copy.start()
        sends.append(copy)

    trail_copy.start()
    @pl.when(jnp.logical_not(has_below))
    def _():
        signal(up_sem, row + 2)

    @pl.when(jnp.logical_not(has_above))
    def _():
        signal(down_sem, row - 2)

    @pl.when(has_below)
    def _():
        pl.semaphore_wait(up_sem, 1)
        pl.when(has_above)(lambda: signal(up_sem, row + 2))

    @pl.when(has_above)
    def _():
        pl.semaphore_wait(down_sem, 1)
        pl.when(has_below)(lambda: signal(down_sem, row - 2))

    signal(mate_sem, mate)
    tc = trail.shape[0]
    acc = jnp.zeros((count, count + tc), F32)
    trail_copy.wait()

    def receive(k):
        window = pl.ds(*windows[k])
        for d in range(1, n_x):
            theirs = mains(x_source(d), window)
            remote(theirs, theirs, xs.at[k, d - 1], xr.at[k, d - 1], (row, x_peer(d))).wait_recv()
            copy = remote(theirs, theirs, fs.at[k, d - 1], fr.at[k, d - 1], (row, sibling))
            copy.start()
            sends.append(copy)
        if heavy is not None:
            @pl.when(is_relay)
            def _():
                more = bufs.at[extra, window]
                remote(more, more, exs.at[k, 0], exr.at[k], (row, x_peer(1))).wait_recv()
                remote(more, more, ess.at[k], esr.at[k], (row, sibling)).start()

    def gathered(k):
        first, width = windows[k]
        window = pl.ds(first, width)
        t_high, t_low = split(trail[:, window])
        arrived = mains(sibling, window)
        remote(arrived, arrived, ss.at[k], sr.at[k], (row, sibling)).wait_recv()
        for d in range(1, n_x):
            arrived = mains(lax.rem(x + n_x - d, n_x) * CORES + (1 - core), window)
            remote(arrived, arrived, fs.at[k, d - 1], fr.at[k, d - 1], (row, sibling)).wait_recv()
        if heavy is not None:
            @pl.when(jnp.logical_not(is_told))
            def _():
                more = bufs.at[extra, window]
                remote(more, more, ess.at[k], esr.at[k], (row, sibling)).wait_recv()
        high, low_part = split(bufs[:, window])
        p_high = dot(expand, high).astype(BF16)
        p_low = dot(expand, low_part).astype(BF16)
        high_ref[:, window] = p_high
        low_ref[:, window] = p_low
        both = dot_t(jnp.concatenate([p_high, p_low], axis=0), jnp.concatenate([p_high, t_high], axis=0))
        return both[:count] + both[count:] + dot_t(p_high, jnp.concatenate([p_low, t_low], axis=0))

    for k in range(len(windows)):
        receive(k)
        if k > 0:
            acc += gathered(k - 1)
    acc += gathered(len(windows) - 1)

    pl.semaphore_wait(mate_sem, 1)
    part = count // n_row
    half = count // 2
    for r in range(n_row):
        csend[r] = acc[r * part:(r + 1) * part, count:]
    crecv[row] = csend[row]
    for d in range(1, n_row):
        copy = remote(csend.at[row_peer(d)], crecv.at[row], cs.at[d - 1], cr.at[d - 1], (row_peer(d), col))
        copy.start()
        sends.append(copy)

    grams[row] = jnp.concatenate([acc[:half, :count], acc[half:, :count]], axis=1)
    for d in range(1, n_row):
        mine = grams.at[row]
        copy = remote(mine, mine, gs.at[d - 1], gr.at[d - 1], (row_peer(d), col))
        copy.start()
        sends.append(copy)
    def source(d):
        return lax.rem(row + n_row - d, n_row)

    for d in range(1, n_row):
        arrived = crecv.at[source(d)]
        remote(arrived, arrived, cs.at[d - 1], cr.at[d - 1], (row_peer(d), col)).wait_recv()
    cfull[row] = jnp.sum(crecv[...], axis=0)
    for d in range(1, n_row):
        mine = cfull.at[row]
        copy = remote(mine, mine, as_.at[d - 1], ar.at[d - 1], (row_peer(d), col))
        copy.start()
        sends.append(copy)
    for d in range(1, n_row):
        arrived = grams.at[source(d)]
        remote(arrived, arrived, gs.at[d - 1], gr.at[d - 1], (row_peer(d), col)).wait_recv()
    packed = jnp.sum(grams[...], axis=0)
    gram = jnp.concatenate([packed[:, :count], packed[:, count:]], axis=0)
    unit = jnp.where(rows_i == lanes_i, 1.0, 0.0)
    state = jnp.concatenate([gram, unit], axis=1)
    done = []
    for start in range(0, count, BLOCK):
        block, state = eliminate(state, start)
        done.append(block)
    state = jnp.concatenate(done, axis=0)
    wide = (count, 2 * count)
    diagonal = jnp.sum(jnp.where(iota(wide, 0) == iota(wide, 1), state, 0.0), axis=1, keepdims=True)
    scaled = state / jnp.sqrt(diagonal)
    factor = jnp.where(iota(wide, 0) <= iota(wide, 1), scaled, 0.0)[:, :count]
    inverse = scaled[:, count:]
    rp_ref[...] = factor * (1.0 / root_rows)
    for d in range(1, n_row):
        arrived = cfull.at[source(d)]
        remote(arrived, arrived, as_.at[d - 1], ar.at[d - 1], (row_peer(d), col)).wait_recv()
    projected = exact(inverse, cfull[...].reshape(count, tc))
    weights = exact(inverse.T, projected).T
    rt_ref[...] = projected * (1.0 / root_rows)
    left_high, left_low = split(jnp.concatenate([inverse * root_rows, weights], axis=0))
    left_ref[...] = jnp.concatenate([left_high, left_low, left_high], axis=1)
    for copy in sends:
        copy.wait_send()
    if heavy is not None:
        for k, (first, width) in enumerate(windows):
            more = bufs.at[extra, pl.ds(first, width)]

            @pl.when(is_heavy)
            def _():
                for d in range(1, n_x):
                    remote(more, more, exs.at[k, d - 1], exr.at[k], (row, x_peer(d))).wait_send()

            @pl.when(is_told)
            def _():
                remote(more, more, ess.at[k], esr.at[k], (row, sibling)).wait_send()


def update_kernel(
    chunks,
    rp_ref, rt_ref, left_ref, high, low, trail,
    rp_hbm, rt_hbm, basis_hbm, next_hbm,
    basis, after,
    small_sem, out_sem,
):
    stores = []
    for i, (src, dst) in enumerate(((rp_ref, rp_hbm), (rt_ref, rt_hbm))):
        copy = pltpu.make_async_copy(src, dst, small_sem.at[i])
        copy.start()
        stores.append(copy)
    count = high.shape[0]
    width = trail.shape[1] // chunks
    left = left_ref[...]
    for k in range(chunks):
        window = pl.ds(k * width, width)
        p_high = high[:, window]
        result = dot(left, jnp.concatenate([p_high, p_high, low[:, window]], axis=0))
        basis[:, window] = result[:count]
        after[:, window] = trail[:, window] - result[count:]
        for i, (src, dst) in enumerate(((basis, basis_hbm), (after, next_hbm))):
            copy = pltpu.make_async_copy(src.at[:, window], dst.at[:, window], out_sem.at[k, i])
            copy.start()
            stores.append(copy)
    for copy in stores:
        copy.wait()


def solution(mesh):
    n_row, n_col = mesh.shape["row"], mesh.shape["col"]
    n_x = n_col // CORES
    chunks = len(PIECES)
    update_chunks = UPDATE_CHUNKS

    def on_device(candidates, trailing, pivots):
        count = pivots.shape[0]
        cand_count = candidates.shape[0]
        low = count // 4
        owner = pivots // cand_count
        index = jnp.int32(n_col)
        ones = jnp.uint32(0)
        for base in range(0, n_col, 4):
            here = (owner >= base) & (owner < base + 4)
            shift = (8 * (owner & 3)).astype(jnp.uint32)
            held = jnp.sum(jnp.where(here, jnp.uint32(1) << shift, jnp.uint32(0)))
            over = (held + jnp.uint32((127 - low) * 0x01010101)) & jnp.uint32(0x80808080)
            for c in range(base, min(base + 4, n_col)):
                alone = (over == jnp.uint32(0x80 << (8 * (c - base)))) & (ones == 0)
                index = jnp.where(alone, c, index)
            index = jnp.where((over != 0) & (ones != 0), n_col, index)
            ones = ones | over
        branches = [functools.partial(step, low, heavy) for heavy in range(n_col)]
        branches.append(functools.partial(step, count // 2, None))
        return lax.switch(index, branches, candidates, trailing, pivots)

    def step(low, heavy, candidates, trailing, pivots):
        cand_count, rows = candidates.shape
        tc = trailing.shape[0]
        count = pivots.shape[0]
        slots = n_col * low + (0 if heavy is None else count // 2 - low)
        unit = rows // sum(PIECES)
        windows = tuple((sum(PIECES[:k]) * unit, PIECES[k] * unit) for k in range(chunks))
        part = count // n_row
        vmem = pl.BlockSpec(memory_space=pltpu.VMEM)
        hbm = pl.BlockSpec(memory_space=pltpu.HBM)
        dma = pltpu.SemaphoreType.DMA
        root_rows = float(rows * n_row) ** 0.5
        handed = pl.pallas_call(
            functools.partial(gather_kernel, n_row, n_col, windows, root_rows, low, heavy),
            name="gather",
            out_shape=(
                jax.ShapeDtypeStruct((count, count), F32),
                jax.ShapeDtypeStruct((count, tc), F32),
                jax.ShapeDtypeStruct((count + tc, 3 * count), BF16),
                jax.ShapeDtypeStruct((count, rows), BF16),
                jax.ShapeDtypeStruct((count, rows), BF16),
                jax.ShapeDtypeStruct((tc, rows), F32),
            ),
            in_specs=[hbm, hbm, hbm],
            out_specs=(vmem,) * 6,
            scratch_shapes=[
                pltpu.VMEM((1, count), jnp.int32),
                pltpu.VMEM((cand_count, rows), F32),
                pltpu.VMEM((slots, rows), F32),
                pltpu.VMEM((n_row, count // 2, 2 * count), F32),
                pltpu.VMEM((n_row, part, tc), F32),
                pltpu.VMEM((n_row, part, tc), F32),
                pltpu.VMEM((n_row, part, tc), F32),
                dma, dma((chunks,)), dma,
                dma((chunks, n_x - 1)), dma((chunks, n_x - 1)),
                dma((chunks,)), dma((chunks,)),
                dma((chunks, n_x - 1)), dma((chunks, n_x - 1)),
                dma((chunks, n_x - 1)), dma((chunks,)), dma((chunks,)), dma((chunks,)),
                dma((n_row - 1,)), dma((n_row - 1,)),
                dma((n_row - 1,)), dma((n_row - 1,)),
                dma((n_row - 1,)), dma((n_row - 1,)),
            ] + [pltpu.SemaphoreType.REGULAR] * 3,
            compiler_params=pltpu.CompilerParams(
                collective_id=n_col if heavy is None else heavy, has_side_effects=True, vmem_limit_bytes=GRANT,
            ),
        )(*[pltpu.with_memory_space_constraint(a, pltpu.HBM) for a in (pivots.reshape(1, count), candidates, trailing)])
        return pl.pallas_call(
            functools.partial(update_kernel, update_chunks),
            name="update",
            out_shape=(
                jax.ShapeDtypeStruct((count, count), F32),
                jax.ShapeDtypeStruct((count, tc), F32),
                jax.ShapeDtypeStruct((count, rows), F32),
                jax.ShapeDtypeStruct((tc, rows), F32),
            ),
            in_specs=[vmem] * 6,
            out_specs=(hbm,) * 4,
            scratch_shapes=[
                pltpu.VMEM((count, rows), F32),
                pltpu.VMEM((tc, rows), F32),
                dma((2,)), dma((update_chunks, 2)),
            ],
            compiler_params=pltpu.CompilerParams(vmem_limit_bytes=GRANT),
        )(*handed)

    placed = (P("col", "row"), P("col", "row"), P())
    return jax.shard_map(
        on_device,
        mesh=mesh,
        in_specs=placed,
        out_specs=(P(), P(None, "col"), P(None, "row"), P("col", "row")),
        check_vma=False,
    )
```

```python
import functools

import jax
import jax.numpy as jnp
from jax import lax
from jax.experimental import pallas as pl
from jax.experimental.pallas import tpu as pltpu
from jax.sharding import PartitionSpec as P

MESH = pl.DeviceIdType.MESH
CORES = 2
F32 = jnp.float32
BF16 = jnp.bfloat16
BLOCK = 16
PIECES = (1, 4, 3)
UPDATE_CHUNKS = 4
GRANT = 24 * 2**20


def split(x):
    high = x.astype(BF16)
    return high, (x - high.astype(F32)).astype(BF16)


def dot(a, b):
    return jnp.dot(a, b, preferred_element_type=F32)


def exact(a, b):
    return jnp.dot(a, b, preferred_element_type=F32, precision=lax.Precision.HIGHEST)


def dot_t(a, b):
    return lax.dot_general(a, b, (((1,), (1,)), ((), ())), preferred_element_type=F32)


def iota(shape, dim):
    return lax.broadcasted_iota(jnp.int32, shape, dim)


def eliminate(state, start):
    rest = state
    tile = iota((BLOCK, state.shape[1]), 0)
    columns = [jnp.broadcast_to(rest[:, start + c:start + c + 1], rest.shape) for c in range(BLOCK)]
    for c in range(BLOCK):
        inverse = 1.0 / columns[c][c:c + 1]
        below = jnp.where(tile > c, columns[c][:BLOCK], 0.0)
        if rest.shape[0] > BLOCK:
            below = jnp.concatenate([below, columns[c][BLOCK:]], axis=0)
        for e in range(c + 1, BLOCK):
            columns[e] = columns[e] - below * (columns[e][c:c + 1] * inverse)
        rest = rest - below * (rest[c:c + 1] * inverse)
    return rest[:BLOCK], rest[BLOCK:]


def gather_kernel(
    n_row, n_col, windows, root_rows, low, heavy,
    piv_hbm, cand_hbm, trail_hbm,
    rp_ref, rt_ref, left_ref, high_ref, low_ref, trail,
    piv_ref, cand, bufs, grams, csend, crecv, cfull,
    piv_sem, cand_sem, trail_sem,
    xs, xr, ss, sr, fs, fr, exs, exr, ess, esr, gs, gr, cs, cr, as_, ar,
    up_sem, down_sem, mate_sem,
):
    row = lax.axis_index("row")
    col = lax.axis_index("col")
    n_x = n_col // CORES
    x = col // CORES
    core = lax.rem(col, CORES)
    sibling = x * CORES + (1 - core)
    count = piv_ref.shape[1]
    cand_count = cand.shape[0]
    slots = bufs.shape[0]
    extra = pl.ds(n_col * low, slots - n_col * low)

    def x_peer(d):
        return lax.rem(x + d, n_x) * CORES + core

    def x_source(d):
        return lax.rem(x + n_x - d, n_x) * CORES + core

    def row_peer(d):
        return lax.rem(row + d, n_row)

    barrier = pltpu.get_barrier_semaphore()
    pl.semaphore_signal(barrier, inc=1, device_id=(row, sibling), device_id_type=MESH)
    for d in range(1, n_x):
        pl.semaphore_signal(barrier, inc=1, device_id=(row, x_peer(d)), device_id_type=MESH)
    mate = row + 1 - 2 * lax.rem(row, 2)
    has_below, has_above = row >= 2, row < n_row - 2

    def signal(semaphore, to):
        pl.semaphore_signal(semaphore, inc=1, device_id=(to, col), device_id_type=MESH)

    signal(barrier, mate)
    pl.when(has_below)(lambda: signal(barrier, row - 2))
    pl.when(has_above)(lambda: signal(barrier, row + 2))

    piv_copy = pltpu.make_async_copy(piv_hbm, piv_ref, piv_sem)
    piv_copy.start()
    cand_copies = []
    for k, (first, width) in enumerate(windows):
        window = pl.ds(first, width)
        copy = pltpu.make_async_copy(cand_hbm.at[:, window], cand.at[:, window], cand_sem.at[k])
        copy.start()
        cand_copies.append(copy)
    trail_copy = pltpu.make_async_copy(trail_hbm, trail, trail_sem)

    piv_copy.wait()
    piv_lane = jnp.broadcast_to(piv_ref[...].astype(F32), (count, count))
    rows_i, lanes_i = iota((count, count), 0), iota((count, count), 1)
    piv_sub = jnp.sum(jnp.where(rows_i == lanes_i, piv_lane, 0.0), axis=1, keepdims=True)
    owner_lane = jnp.zeros((count, count), F32)
    owner_sub = jnp.zeros((count, 1), F32)
    for s in range(1, n_col):
        owner_lane += (piv_lane >= s * cand_count).astype(F32)
        owner_sub += (piv_sub >= s * cand_count).astype(F32)
    same = jnp.broadcast_to(owner_sub, (count, count)) == owner_lane
    rank_sub = jnp.sum(jnp.where(same & (lanes_i < rows_i), 1.0, 0.0), axis=1, keepdims=True)
    rank_lane = jnp.sum(jnp.where(same & (rows_i < lanes_i), 1.0, 0.0), axis=0, keepdims=True)
    def slot_of(owner, rank):
        return jnp.where(rank < low, owner * low + rank, rank + (n_col - 1) * low).astype(jnp.int32)

    expand = (slot_of(owner_sub, rank_sub) == iota((count, slots), 1)).astype(F32).astype(BF16)
    own = iota((slots - (n_col - 1) * low, count), 0)
    own = jnp.where(own < low, own + col * low, own + (n_col - 1) * low)
    to_slot = (slot_of(owner_lane[:1], rank_lane) == own).astype(F32).astype(BF16)
    to_cand = (piv_sub.astype(jnp.int32) == col * cand_count + iota((count, cand_count), 1))
    pick = dot(to_slot, to_cand.astype(F32).astype(BF16)).astype(BF16)

    def remote(src, dst, send, recv, device):
        return pltpu.make_async_remote_copy(
            src_ref=src, dst_ref=dst, send_sem=send, recv_sem=recv,
            device_id=device, device_id_type=MESH,
        )

    def mains(owner, window):
        return bufs.at[pl.ds(pl.multiple_of(owner * low, low), low), window]

    sends = []
    if heavy is not None:
        heavy_x, heavy_core = heavy // CORES, heavy % CORES
        is_heavy = col == heavy
        is_relay = (core == heavy_core) & (x != heavy_x)
        is_told = core == heavy_core

    for k, (first, width) in enumerate(windows):
        window = pl.ds(first, width)
        cand_copies[k].wait()
        high, low_part = split(cand[:, window])
        picked = dot(pick, high) + dot(pick, low_part)
        bufs[pl.ds(pl.multiple_of(col * low, low), low), window] = picked[:low]
        if k == 0:
            pl.semaphore_wait(barrier, n_x + 1 + has_below.astype(jnp.int32) + has_above.astype(jnp.int32))
        mine = mains(col, window)
        for d in range(1, n_x):
            copy = remote(mine, mine, xs.at[k, d - 1], xr.at[k, d - 1], (row, x_peer(d)))
            copy.start()
            sends.append(copy)
        if heavy is not None:
            @pl.when(is_heavy)
            def _():
                bufs[extra, window] = picked[low:]
                more = bufs.at[extra, window]
                for d in range(1, n_x):
                    remote(more, more, exs.at[k, d - 1], exr.at[k], (row, x_peer(d))).start()
                remote(more, more, ess.at[k], esr.at[k], (row, sibling)).start()
        copy = remote(mine, mine, ss.at[k], sr.at[k], (row, sibling))
        copy.start()
        sends.append(copy)
        if k == 0:
            signal(mate_sem, mate)

            @pl.when(jnp.logical_not(has_below))
            def _():
                signal(up_sem, row + 2)

            @pl.when(jnp.logical_not(has_above))
            def _():
                signal(down_sem, row - 2)

    trail_copy.start()
    @pl.when(has_below)
    def _():
        pl.semaphore_wait(up_sem, 1)
        pl.when(has_above)(lambda: signal(up_sem, row + 2))

    @pl.when(has_above)
    def _():
        pl.semaphore_wait(down_sem, 1)
        pl.when(has_below)(lambda: signal(down_sem, row - 2))

    tc = trail.shape[0]
    acc = jnp.zeros((count, count + tc), F32)
    trail_copy.wait()

    def receive(k):
        window = pl.ds(*windows[k])
        for d in range(1, n_x):
            theirs = mains(x_source(d), window)
            remote(theirs, theirs, xs.at[k, d - 1], xr.at[k, d - 1], (row, x_peer(d))).wait_recv()
            copy = remote(theirs, theirs, fs.at[k, d - 1], fr.at[k, d - 1], (row, sibling))
            copy.start()
            sends.append(copy)
        if heavy is not None:
            @pl.when(is_relay)
            def _():
                more = bufs.at[extra, window]
                remote(more, more, exs.at[k, 0], exr.at[k], (row, x_peer(1))).wait_recv()
                remote(more, more, ess.at[k], esr.at[k], (row, sibling)).start()

    def gathered(k):
        first, width = windows[k]
        window = pl.ds(first, width)
        t_high, t_low = split(trail[:, window])
        arrived = mains(sibling, window)
        remote(arrived, arrived, ss.at[k], sr.at[k], (row, sibling)).wait_recv()
        for d in range(1, n_x):
            arrived = mains(lax.rem(x + n_x - d, n_x) * CORES + (1 - core), window)
            remote(arrived, arrived, fs.at[k, d - 1], fr.at[k, d - 1], (row, sibling)).wait_recv()
        if heavy is not None:
            @pl.when(jnp.logical_not(is_told))
            def _():
                more = bufs.at[extra, window]
                remote(more, more, ess.at[k], esr.at[k], (row, sibling)).wait_recv()
        high, low_part = split(bufs[:, window])
        p_high = dot(expand, high).astype(BF16)
        p_low = dot(expand, low_part).astype(BF16)
        high_ref[:, window] = p_high
        low_ref[:, window] = p_low
        both = dot_t(jnp.concatenate([p_high, p_low], axis=0), jnp.concatenate([p_high, t_high], axis=0))
        return both[:count] + both[count:] + dot_t(p_high, jnp.concatenate([p_low, t_low], axis=0))

    for k in range(len(windows)):
        receive(k)
        if k > 0:
            acc += gathered(k - 1)
    acc += gathered(len(windows) - 1)

    pl.semaphore_wait(mate_sem, 1)
    part = count // n_row
    half = count // 2
    for r in range(n_row):
        csend[r] = acc[r * part:(r + 1) * part, count:]
    crecv[row] = csend[row]
    for d in range(1, n_row):
        copy = remote(csend.at[row_peer(d)], crecv.at[row], cs.at[d - 1], cr.at[d - 1], (row_peer(d), col))
        copy.start()
        sends.append(copy)

    grams[row] = jnp.concatenate([acc[:half, :count], acc[half:, :count]], axis=1)
    for d in range(1, n_row):
        mine = grams.at[row]
        copy = remote(mine, mine, gs.at[d - 1], gr.at[d - 1], (row_peer(d), col))
        copy.start()
        sends.append(copy)
    def source(d):
        return lax.rem(row + n_row - d, n_row)

    for d in range(1, n_row):
        arrived = crecv.at[source(d)]
        remote(arrived, arrived, cs.at[d - 1], cr.at[d - 1], (row_peer(d), col)).wait_recv()
    cfull[row] = jnp.sum(crecv[...], axis=0)
    for d in range(1, n_row):
        mine = cfull.at[row]
        copy = remote(mine, mine, as_.at[d - 1], ar.at[d - 1], (row_peer(d), col))
        copy.start()
        sends.append(copy)
    for d in range(1, n_row):
        arrived = grams.at[source(d)]
        remote(arrived, arrived, gs.at[d - 1], gr.at[d - 1], (row_peer(d), col)).wait_recv()
    packed = jnp.sum(grams[...], axis=0)
    gram = jnp.concatenate([packed[:, :count], packed[:, count:]], axis=0)
    unit = jnp.where(rows_i == lanes_i, 1.0, 0.0)
    state = jnp.concatenate([gram, unit], axis=1)
    done = []
    for start in range(0, count, BLOCK):
        block, state = eliminate(state, start)
        done.append(block)
    state = jnp.concatenate(done, axis=0)
    wide = (count, 2 * count)
    diagonal = jnp.sum(jnp.where(iota(wide, 0) == iota(wide, 1), state, 0.0), axis=1, keepdims=True)
    scaled = state / jnp.sqrt(diagonal)
    factor = jnp.where(iota(wide, 0) <= iota(wide, 1), scaled, 0.0)[:, :count]
    inverse = scaled[:, count:]
    rp_ref[...] = factor * (1.0 / root_rows)
    for d in range(1, n_row):
        arrived = cfull.at[source(d)]
        remote(arrived, arrived, as_.at[d - 1], ar.at[d - 1], (row_peer(d), col)).wait_recv()
    projected = exact(inverse, cfull[...].reshape(count, tc))
    weights = exact(inverse.T, projected).T
    rt_ref[...] = projected * (1.0 / root_rows)
    left_high, left_low = split(jnp.concatenate([inverse * root_rows, weights], axis=0))
    left_ref[...] = jnp.concatenate([left_high, left_low, left_high], axis=1)
    for copy in sends:
        copy.wait_send()
    if heavy is not None:
        for k, (first, width) in enumerate(windows):
            more = bufs.at[extra, pl.ds(first, width)]

            @pl.when(is_heavy)
            def _():
                for d in range(1, n_x):
                    remote(more, more, exs.at[k, d - 1], exr.at[k], (row, x_peer(d))).wait_send()

            @pl.when(is_told)
            def _():
                remote(more, more, ess.at[k], esr.at[k], (row, sibling)).wait_send()


def update_kernel(
    chunks,
    rp_ref, rt_ref, left_ref, high, low, trail,
    rp_hbm, rt_hbm, basis_hbm, next_hbm,
    basis, after,
    small_sem, out_sem,
):
    stores = []
    for i, (src, dst) in enumerate(((rp_ref, rp_hbm), (rt_ref, rt_hbm))):
        copy = pltpu.make_async_copy(src, dst, small_sem.at[i])
        copy.start()
        stores.append(copy)
    count = high.shape[0]
    width = trail.shape[1] // chunks
    left = left_ref[...]
    for k in range(chunks):
        window = pl.ds(k * width, width)
        p_high = high[:, window]
        result = dot(left, jnp.concatenate([p_high, p_high, low[:, window]], axis=0))
        basis[:, window] = result[:count]
        after[:, window] = trail[:, window] - result[count:]
        for i, (src, dst) in enumerate(((basis, basis_hbm), (after, next_hbm))):
            copy = pltpu.make_async_copy(src.at[:, window], dst.at[:, window], out_sem.at[k, i])
            copy.start()
            stores.append(copy)
    for copy in stores:
        copy.wait()


def solution(mesh):
    n_row, n_col = mesh.shape["row"], mesh.shape["col"]
    n_x = n_col // CORES
    chunks = len(PIECES)
    update_chunks = UPDATE_CHUNKS

    def on_device(candidates, trailing, pivots):
        count = pivots.shape[0]
        cand_count = candidates.shape[0]
        low = count // 4
        owner = pivots // cand_count
        index = jnp.int32(n_col)
        ones = jnp.uint32(0)
        for base in range(0, n_col, 4):
            here = (owner >= base) & (owner < base + 4)
            shift = (8 * (owner & 3)).astype(jnp.uint32)
            held = jnp.sum(jnp.where(here, jnp.uint32(1) << shift, jnp.uint32(0)))
            over = (held + jnp.uint32((127 - low) * 0x01010101)) & jnp.uint32(0x80808080)
            for c in range(base, min(base + 4, n_col)):
                alone = (over == jnp.uint32(0x80 << (8 * (c - base)))) & (ones == 0)
                index = jnp.where(alone, c, index)
            index = jnp.where((over != 0) & (ones != 0), n_col, index)
            ones = ones | over
        branches = [functools.partial(step, low, heavy) for heavy in range(n_col)]
        branches.append(functools.partial(step, count // 2, None))
        handed = lax.switch(index, branches, candidates, trailing, pivots)
        rows, tc = candidates.shape[1], trailing.shape[0]
        vmem = pl.BlockSpec(memory_space=pltpu.VMEM)
        hbm = pl.BlockSpec(memory_space=pltpu.HBM)
        dma = pltpu.SemaphoreType.DMA
        return pl.pallas_call(
            functools.partial(update_kernel, update_chunks),
            name="update",
            out_shape=(
                jax.ShapeDtypeStruct((count, count), F32),
                jax.ShapeDtypeStruct((count, tc), F32),
                jax.ShapeDtypeStruct((count, rows), F32),
                jax.ShapeDtypeStruct((tc, rows), F32),
            ),
            in_specs=[vmem] * 6,
            out_specs=(hbm,) * 4,
            scratch_shapes=[
                pltpu.VMEM((count, rows), F32),
                pltpu.VMEM((tc, rows), F32),
                dma((2,)), dma((update_chunks, 2)),
            ],
            compiler_params=pltpu.CompilerParams(vmem_limit_bytes=GRANT),
        )(*handed)


    def step(low, heavy, candidates, trailing, pivots):
        cand_count, rows = candidates.shape
        tc = trailing.shape[0]
        count = pivots.shape[0]
        slots = n_col * low + (0 if heavy is None else count // 2 - low)
        unit = rows // sum(PIECES)
        windows = tuple((sum(PIECES[:k]) * unit, PIECES[k] * unit) for k in range(chunks))
        part = count // n_row
        vmem = pl.BlockSpec(memory_space=pltpu.VMEM)
        hbm = pl.BlockSpec(memory_space=pltpu.HBM)
        dma = pltpu.SemaphoreType.DMA
        root_rows = float(rows * n_row) ** 0.5
        handed = pl.pallas_call(
            functools.partial(gather_kernel, n_row, n_col, windows, root_rows, low, heavy),
            name="gather",
            out_shape=(
                jax.ShapeDtypeStruct((count, count), F32),
                jax.ShapeDtypeStruct((count, tc), F32),
                jax.ShapeDtypeStruct((count + tc, 3 * count), BF16),
                jax.ShapeDtypeStruct((count, rows), BF16),
                jax.ShapeDtypeStruct((count, rows), BF16),
                jax.ShapeDtypeStruct((tc, rows), F32),
            ),
            in_specs=[hbm, hbm, hbm],
            out_specs=(vmem,) * 6,
            scratch_shapes=[
                pltpu.VMEM((1, count), jnp.int32),
                pltpu.VMEM((cand_count, rows), F32),
                pltpu.VMEM((slots, rows), F32),
                pltpu.VMEM((n_row, count // 2, 2 * count), F32),
                pltpu.VMEM((n_row, part, tc), F32),
                pltpu.VMEM((n_row, part, tc), F32),
                pltpu.VMEM((n_row, part, tc), F32),
                dma, dma((chunks,)), dma,
                dma((chunks, n_x - 1)), dma((chunks, n_x - 1)),
                dma((chunks,)), dma((chunks,)),
                dma((chunks, n_x - 1)), dma((chunks, n_x - 1)),
                dma((chunks, n_x - 1)), dma((chunks,)), dma((chunks,)), dma((chunks,)),
                dma((n_row - 1,)), dma((n_row - 1,)),
                dma((n_row - 1,)), dma((n_row - 1,)),
                dma((n_row - 1,)), dma((n_row - 1,)),
            ] + [pltpu.SemaphoreType.REGULAR] * 3,
            compiler_params=pltpu.CompilerParams(
                collective_id=n_col if heavy is None else heavy, has_side_effects=True, vmem_limit_bytes=GRANT,
            ),
        )(*[pltpu.with_memory_space_constraint(a, pltpu.HBM) for a in (pivots.reshape(1, count), candidates, trailing)])
        return handed

    placed = (P("col", "row"), P("col", "row"), P())
    return jax.shard_map(
        on_device,
        mesh=mesh,
        in_specs=placed,
        out_specs=(P(), P(None, "col"), P(None, "row"), P("col", "row")),
        check_vma=False,
    )
```
